512 devices in a mesh: wide: 64 (over z, x), narrow: 8 (over y, core).
Axes of the slice: x: 4, y: 4, z: 16, core: 2. Of those that a mesh axis runs over, the one named last changes fastest.
Arguments:
- hidden: bfloat16 [2048, 8192], P('wide', 'narrow'), may hold values from -6 to 6
- norm_gain: float32 [8192], P('narrow'), may hold values from 0.1 to 1.9
- head_weight: bfloat16 [8192, 32000], P('narrow', 'wide'), may hold values from -0.24 to 0.24
- diff_rows: bfloat16 [64, 8, 8, 32000], P('wide', 'narrow'), may hold values from -6 to 480
- slot_request: int32 [64, 8, 8], replicated, may hold values from 0 to 2047, as said below
- slot_code: int32 [64, 8, 8], replicated, may hold values from 1 to 8
- slot_count: int32 [64, 8], replicated, may hold values from 1 to 8, as said below
Outputs:
- log_probs: float32 [2048, 32000], P('narrow', 'wide')
The draws below stay inside these ranges and needn't reach their ends.
Inputs may be any that keep to these rules, and one draw needn't show every extreme that they name: `slot_request`: within one pair, every request is named at most once. `slot_count`: slots at or beyond the count hold no row to use; in every draw some device uses all 8 slots.
All inputs are finite; a program needn't handle non-finite values.
Results may differ from the reference program's by a relative error of at most 0.0003.
Values may be sent and summed in bfloat16 or wider, within the bound.
A program may use at most 64 MiB of HBM per device.

```python
import jax
import jax.numpy as jnp
from jax import lax

D = 8192
VOCAB = 32000
REQ_DEV = 32
CAP = 8
REQUESTS = 2048
PAIRS = 64
N_WIDE = 64
N_NARROW = 8


def state_values(key):
    return jnp.clip(jax.random.normal(jax.random.fold_in(key, 11), (REQUESTS, D), jnp.float32), -6.0, 6.0)


def draw_hidden(key, part):
    return state_values(key).astype(jnp.bfloat16)


def draw_head_weight(key, part):
    key_weight = jax.random.fold_in(key, 23)
    return jnp.clip(0.04 * jax.random.normal(key_weight, (D, VOCAB), jnp.float32), -0.24, 0.24).astype(jnp.bfloat16)


def draw_diff_rows(key, part):
    key_values = jax.random.fold_in(key, 0)
    shape = (N_WIDE, N_NARROW, CAP, VOCAB)
    return jnp.clip(jax.random.normal(key_values, shape, jnp.float32), -6.0, 6.0).astype(jnp.bfloat16)


def permute(pair_key):
    return jax.random.permutation(pair_key, REQ_DEV * N_WIDE)[:N_NARROW * CAP]


def draw_slot_request(key, part):
    total = REQ_DEV * N_WIDE
    pair_keys = jax.random.split(key, N_WIDE)
    orders = jax.vmap(permute)(pair_keys).astype(jnp.int32)
    groups = jnp.arange(N_WIDE, dtype=jnp.int32)[:, None]
    target = jnp.where(groups == 0, total - 1, jnp.where(groups == 1, 0, orders[:, :1]))
    chosen = (orders + target - orders[:, :1]) % total
    return chosen.reshape(N_WIDE, N_NARROW, CAP).astype(jnp.int32)


def draw_slot_count(key, part):
    key_first, key_second, key_full = jax.random.split(key, 3)
    first_draw = jax.random.randint(key_first, (N_WIDE, N_NARROW), 0, CAP)
    second_draw = jax.random.randint(key_second, (N_WIDE, N_NARROW), 0, CAP)
    divisor = max(1, CAP // 2)
    counts = jnp.minimum(CAP, 1 + first_draw * second_draw // divisor).reshape(-1)
    full_slot = jax.random.randint(key_full, (), 0, N_WIDE * N_NARROW)
    counts = jnp.where(jnp.arange(N_WIDE * N_NARROW, dtype=jnp.int32) == full_slot, CAP, counts)
    return counts.reshape(N_WIDE, N_NARROW).astype(jnp.int32)


def touch_ends(drawn, key, smallest, high):
    longest = drawn.shape.index(max(drawn.shape))
    spots = []
    for shift in (0, 1):
        where = [jax.random.randint(jax.random.fold_in(key, axis), (), 0, length) for axis, length in enumerate(drawn.shape)]
        where[longest] = (where[longest] + shift) % drawn.shape[longest]
        spots.append(tuple(where))
    return drawn.at[spots[0]].set(smallest).at[spots[1]].set(high)


def setup_inputs(seed: int = 0) -> dict:
    keys = jax.random.split(jax.random.key(seed), 8)
    hidden = draw_hidden(jax.random.fold_in(keys[7], 71), 0)
    norm_gain = jnp.clip(1.0 + 0.18 * jax.random.normal(keys[1], (D,), jnp.float32), 0.1, 1.9)
    head_weight = draw_head_weight(jax.random.fold_in(keys[7], 71), 0)
    diff_rows = draw_diff_rows(jax.random.fold_in(keys[7], 71), 0)
    slot_request = draw_slot_request(jax.random.fold_in(keys[7], 71), 0)
    slot_code = touch_ends(jax.random.randint(keys[5], (PAIRS, N_NARROW, CAP), 1, 9), jax.random.fold_in(keys[5], 1), 1, 8).astype(jnp.int32)
    slot_count = draw_slot_count(jax.random.fold_in(keys[7], 71), 0)
    return dict(hidden=hidden, norm_gain=norm_gain, head_weight=head_weight, diff_rows=diff_rows, slot_request=slot_request, slot_code=slot_code, slot_count=slot_count)


epsilon = 1e-05

def reference(hidden, norm_gain, head_weight, diff_rows, slot_request, slot_code, slot_count):
    values = hidden.astype(jnp.float32)
    scales = lax.rsqrt(lax.optimization_barrier(jnp.mean(values * values, axis=1, keepdims=True)) + epsilon)
    normed = (values * scales * norm_gain[None, :]).astype(jnp.bfloat16)
    logits = jnp.dot(normed, head_weight, preferred_element_type=jnp.float32)
    active = jnp.arange(CAP, dtype=jnp.int32)[None, None, :] < slot_count[:, :, None]
    factors = jnp.where(active, slot_code, 0).astype(jnp.float32) * 0.25

    def add_group(running, element):
        row_block, requests, weights = element
        weighted = row_block.reshape(-1, VOCAB).astype(jnp.float32) * weights.reshape(-1)[:, None]
        return (running.at[requests.reshape(-1)].add(weighted), None)
    logits, _ = lax.scan(add_group, logits, (diff_rows, slot_request, factors))
    row_peak = lax.optimization_barrier(jnp.max(logits, axis=1, keepdims=True))
    log_total = row_peak + jnp.log(lax.optimization_barrier(jnp.sum(jnp.exp(logits - row_peak), axis=1, keepdims=True)))
    return logits - log_total
```

```python
import functools

import jax
import jax.numpy as jnp
from jax import lax
from jax.experimental import pallas as pl
from jax.experimental.pallas import tpu as pltpu
from jax.sharding import PartitionSpec as P

D = 8192
EPS = 1e-05
NZ, NX, NY, NC = 16, 4, 4, 2
NW, NN = NZ * NX, NY * NC
REQ = 32
ROWS = 256
VOC = 500
PADV = 512
CAP = 8
SLOTS = NW * CAP

f32 = jnp.float32
bf16 = jnp.bfloat16
NT = (((1,), (1,)), ((), ()))


def remote(src, dst, send, recv, wide, narrow):
    return pltpu.make_async_remote_copy(
        src_ref=src,
        dst_ref=dst,
        send_sem=send,
        recv_sem=recv,
        device_id={"wide": wide, "narrow": narrow},
        device_id_type=pl.DeviceIdType.MESH,
    )


def head_kernel(
    h_ref, g_ref, wt_ref, rows_ref, code_ref, o_ref,
    act, recv_rows, rows_t, part, pair, half, full, sq, peaks_x, peaks_z,
    sq_send, sq_recv, a2a_send, a2a_recv, z_send, z_recv, x_send, x_recv, h_send, h_recv,
    p_send, p_recv, y_send, y_recv, sx_send, sx_recv, sz_send, sz_recv,
):
    w = lax.axis_index("wide")
    n = lax.axis_index("narrow")
    z, x, y, c = w // NX, w % NX, n // NC, n % NC

    def wide_of(dz, dx):
        return ((z + dz + NZ) % NZ) * NX + (x + dx + NX) % NX

    values = h_ref[...].astype(f32)
    sq[n] = jnp.broadcast_to(jnp.sum(values * values, axis=1, keepdims=True), (REQ, 128))

    def sq_copy(k):
        return remote(sq.at[n], sq.at[n], sq_send.at[k], sq_recv.at[k], w, (n + k) % NN)

    def sq_arrival(k):
        peer = (n - k + NN) % NN
        return remote(sq.at[peer], sq.at[peer], sq_send.at[k], sq_recv.at[k], w, peer)

    for k in range(1, NN):
        sq_copy(k).start()

    def a2a_copy(k):
        target = (w + k) % NW
        return remote(rows_ref.at[target], recv_rows.at[w], a2a_send, a2a_recv, target, n)

    def a2a_some(first, last):
        @pl.loop(first, last)
        def _(k):
            a2a_copy(k).start()

    a2a_some(1, 8)
    recv_rows[w] = rows_ref[w]

    for k in range(1, NN):
        sq_arrival(k).wait_recv()
    total = jnp.sum(sq[...], axis=0)[:, :1]
    scales = lax.rsqrt(total / D + EPS)
    act[w] = (values * scales * g_ref[...]).astype(bf16)

    top, bottom = pl.ds(0, REQ // 2), pl.ds(REQ // 2, REQ // 2)

    def z_copy(side, d, rows=None):
        step = 1 if side == 0 else -1
        block = act.at[wide_of(-step * d, 0)]
        block = block if rows is None else block.at[rows]
        return remote(block, block, z_send, z_recv.at[side, d + 1], wide_of(step, 0), n)

    def z_arrival(side, d, rows=None):
        step = 1 if side == 0 else -1
        block = act.at[wide_of(-step * d, 0)]
        block = block if rows is None else block.at[rows]
        return remote(block, block, z_send, z_recv.at[side, d], wide_of(step, 0), n)

    def x_copy(side, q, dz):
        step = 1 if side == 0 else -1
        block = act.at[wide_of(dz, 0)]
        return remote(block, block, x_send, x_recv.at[side, q], wide_of(0, step), n)

    def x_arrival(side, q, dz):
        step = 1 if side == 0 else -1
        block = act.at[wide_of(dz, -step)]
        return remote(block, block, x_send, x_recv.at[side, q], wide_of(0, step), n)

    def h_copy(side, q, dz):
        step = 1 if side == 0 else -1
        block = act.at[wide_of(dz, -step)].at[top if side == 0 else bottom]
        return remote(block, block, h_send, h_recv.at[side, q], wide_of(0, step), n)

    def h_arrival(side, q, dz):
        step = 1 if side == 0 else -1
        block = act.at[wide_of(dz, 2)].at[top if side == 0 else bottom]
        return remote(block, block, h_send, h_recv.at[side, q], wide_of(0, step), n)

    events = [[(0, 0)]] + [[(2 * d - 1, -d), (2 * d, d)] for d in range(1, 8)] + [[(15, 8)]]

    def forward_x(d):
        for q, dz in events[d]:
            for side in range(2):
                x_arrival(side, q, dz).wait_recv()
                h_copy(side, q, dz).start()

    LAG = 1
    for d in range(9):
        if d in range(1, 8):
            for side in range(2):
                z_arrival(side, d).wait_recv()
        if d == 8:
            z_arrival(0, 8, top).wait_recv()
            z_arrival(1, 8, bottom).wait_recv()
        if d < 7:
            for side in range(2):
                z_copy(side, d).start()
        if d == 7:
            z_copy(0, 7, top).start()
            z_copy(1, 7, bottom).start()
        for q, dz in events[d]:
            for side in range(2):
                x_copy(side, q, dz).start()
        if d < 8:
            a2a_some(8 + 7 * d, 15 + 7 * d)
        if d >= LAG:
            forward_x(d - LAG)
    for d in range(9 - LAG, 9):
        forward_x(d)
    for d in range(9):
        for q, dz in events[d]:
            for side in range(2):
                h_arrival(side, q, dz).wait_recv()

    pltpu.make_async_copy(rows_ref.at[pl.ds(0, NW - 1)], recv_rows.at[pl.ds(0, NW - 1)], a2a_recv).wait()
    rows_t[...] = jnp.transpose(recv_rows[...].reshape(SLOTS, PADV))

    code = code_ref[...]
    requests = code // 16
    quarters = (code % 16).astype(f32) * 0.25

    def product(block):
        requested = lax.broadcasted_iota(jnp.int32, (ROWS, SLOTS), 0) + block * ROWS
        chosen = jnp.where(requests == requested, quarters, 0.0).astype(bf16)
        left = act[pl.ds(block * (ROWS // REQ), ROWS // REQ)].reshape(ROWS, D // NN)
        part[block] = lax.dot_general(wt_ref[...], left, NT, preferred_element_type=f32) + lax.dot_general(
            rows_t[pl.ds(0, VOC)], chosen, NT, preferred_element_type=f32
        )

    def mine(r):
        return ((y + r) % NY) * NC + c

    def theirs(r):
        return ((y + r) % NY) * NC + 1 - c

    def pair_copy(r):
        return remote(part.at[theirs(r)], pair.at[r], p_send.at[r], p_recv.at[r], w, y * NC + 1 - c)

    def north(k):
        return ((y + k + NY) % NY) * NC + c

    lanes = (pl.ds(0, ROWS // 2), pl.ds(ROWS // 2, ROWS // 2))

    def half_copy(side):
        step = 1 if side == 0 else -1
        return remote(
            part.at[mine(2)].at[:, lanes[side]], half.at[side], y_send.at[side], y_recv.at[side], w, north(step)
        )

    def full_copy(side):
        step = 1 if side == 0 else -1
        return remote(part.at[mine(step % NY)], full.at[side], y_send.at[2 + side], y_recv.at[2 + side], w, north(step))

    order = (2, 1, 3, 0)
    for r in order:
        product(theirs(r))
        pair_copy(r).start()
    for r in order:
        block = mine(r)
        product(block)
        pair_copy(r).wait_recv()
        part[block] += pair[r]
        if r == 2:
            half_copy(0).start()
            half_copy(1).start()
    for side in range(2):
        block = mine(1 if side == 0 else 3)
        half_copy(side).wait_recv()
        part[block, :, lanes[side]] += half[side]
        full_copy(side).start()
    for side in range(2):
        full_copy(side).wait_recv()
    logits = part[mine(0)] + full[0] + full[1]

    def merged(buffer):
        peaks, masses = buffer[:, 0:1, :], buffer[:, 4:5, :]
        peak = jnp.max(peaks, axis=0)
        return peak, jnp.sum(masses * jnp.exp(peaks - peak[None]), axis=0)

    def put(buffer, index, peak, mass):
        buffer[index, 0:4, :] = jnp.broadcast_to(peak, (4, ROWS))
        buffer[index, 4:8, :] = jnp.broadcast_to(mass, (4, ROWS))

    peak = jnp.max(logits, axis=0, keepdims=True)
    mass = jnp.sum(jnp.exp(logits - peak), axis=0, keepdims=True)
    put(peaks_x, x, peak, mass)

    def sx_copy(k):
        return remote(peaks_x.at[x], peaks_x.at[x], sx_send.at[k], sx_recv.at[k], wide_of(0, k), n)

    for k in range(1, NX):
        sx_copy(k).start()
    for k in range(1, NX):
        sx_copy(k).wait_recv()
    peak, mass = merged(peaks_x)
    put(peaks_z, z, peak, mass)

    def sz_copy(k):
        return remote(peaks_z.at[z], peaks_z.at[z], sz_send.at[k], sz_recv.at[k], wide_of(k, 0), n)

    for k in range(1, NZ):
        sz_copy(k).start()
    for k in range(1, NZ):
        sz_copy(k).wait_recv()
    peak, mass = merged(peaks_z)
    o_ref[...] = logits - (peak + jnp.log(mass))

    for k in range(1, NN):
        sq_copy(k).wait_send()
    pltpu.make_async_copy(rows_ref.at[pl.ds(0, NW - 1)], recv_rows.at[pl.ds(0, NW - 1)], a2a_send).wait()
    pltpu.make_async_copy(act.at[pl.ds(0, 15)], act.at[pl.ds(0, 15)], z_send).wait()
    pltpu.make_async_copy(act.at[pl.ds(0, 32)], act.at[pl.ds(0, 32)], x_send).wait()
    pltpu.make_async_copy(act.at[pl.ds(0, 16)], act.at[pl.ds(0, 16)], h_send).wait()
    for r in range(NY):
        pair_copy(r).wait_send()
    for side in range(2):
        half_copy(side).wait_send()
        full_copy(side).wait_send()
    for k in range(1, NX):
        sx_copy(k).wait_send()
    for k in range(1, NZ):
        sz_copy(k).wait_send()


def body(hidden, norm_gain, head_weight, diff_rows, slot_request, slot_code, slot_count):
    n = lax.axis_index("narrow")
    rows = jnp.transpose(diff_rows[0, 0].reshape(CAP, NW, VOC), (1, 0, 2))
    rows = jnp.pad(rows, ((0, 0), (0, 0), (0, PADV - VOC)))
    live = jnp.arange(CAP, dtype=jnp.int32)[None, None, :] < slot_count[:, :, None]
    coded = slot_request * 16 + jnp.where(live, slot_code, 0)
    code = lax.dynamic_index_in_dim(coded, n, 1, False).reshape(1, SLOTS)
    dma = pltpu.SemaphoreType.DMA
    vmem = pl.BlockSpec(memory_space=pltpu.VMEM)
    out = pl.pallas_call(
        head_kernel,
        name="head",
        out_shape=jax.ShapeDtypeStruct((VOC, ROWS), f32),
        in_specs=[vmem] * 5,
        out_specs=vmem,
        scratch_shapes=[
            pltpu.VMEM((NW, REQ, D // NN), bf16),
            pltpu.VMEM((NW, CAP, PADV), bf16),
            pltpu.VMEM((PADV, SLOTS), bf16),
            pltpu.VMEM((NN, VOC, ROWS), f32),
            pltpu.VMEM((NY, VOC, ROWS), f32),
            pltpu.VMEM((2, VOC, ROWS // 2), f32),
            pltpu.VMEM((2, VOC, ROWS), f32),
            pltpu.VMEM((NN, REQ, 128), f32),
            pltpu.VMEM((NX, 8, ROWS), f32),
            pltpu.VMEM((NZ, 8, ROWS), f32),
            dma((NN,)), dma((NN,)), dma, dma, dma, dma((2, 9)), dma, dma((2, 16)), dma, dma((2, 16)),
            dma((NY,)), dma((NY,)), dma((4,)), dma((4,)), dma((NX,)), dma((NX,)), dma((NZ,)), dma((NZ,)),
        ],
        compiler_params=pltpu.CompilerParams(has_side_effects=True, vmem_limit_bytes=40 << 20),
    )(hidden, norm_gain[None, :], head_weight.T, rows, code)
    return out.T


def solution(mesh):
    placed = (
        P("wide", "narrow"),
        P("narrow"),
        P("narrow", "wide"),
        P("wide", "narrow", None, None),
        P(),
        P(),
        P(),
    )
    return jax.shard_map(
        body, mesh=mesh, in_specs=placed, out_specs=P("narrow", "wide"), check_vma=False
    )
```

```python
import functools

import jax
import jax.numpy as jnp
from jax import lax
from jax.experimental import pallas as pl
from jax.experimental.pallas import tpu as pltpu
from jax.sharding import PartitionSpec as P

D = 8192
EPS = 1e-05
NZ, NX, NY, NC = 16, 4, 4, 2
NW, NN = NZ * NX, NY * NC
REQ = 32
ROWS = 256
VOC = 500
PADV = 512
CAP = 8
SLOTS = NW * CAP
FAR = (8, 7, 9, 6, 10, 5, 11, 4, 12, 3, 13, 2, 14, 1, 15)

f32 = jnp.float32
bf16 = jnp.bfloat16
NT = (((1,), (1,)), ((), ()))


def remote(src, dst, send, recv, wide, narrow):
    return pltpu.make_async_remote_copy(
        src_ref=src,
        dst_ref=dst,
        send_sem=send,
        recv_sem=recv,
        device_id={"wide": wide, "narrow": narrow},
        device_id_type=pl.DeviceIdType.MESH,
    )


def head_kernel(
    h_ref, g_ref, wt_ref, diff_ref, req_ref, code_ref, count_ref, o_ref,
    act, bundle, relay, recv_rows, rows_t, part, pair, half, full, sq, peaks_x, peaks_z,
    sq_send, sq_recv, b_send, b_recv, a2a_send, a2a_recv, z_send, z_recv, x_send, x_recv, h_send, h_recv,
    p_send, p_recv, y_send, y_recv, sx_send, sx_recv, sz_send, sz_recv,
):
    w = lax.axis_index("wide")
    n = lax.axis_index("narrow")
    z, x, y, c = w // NX, w % NX, n // NC, n % NC

    def wide_of(dz, dx):
        return ((z + dz + NZ) % NZ) * NX + (x + dx + NX) % NX

    barrier = pltpu.get_barrier_semaphore()

    def greet(wide, narrow):
        pl.semaphore_signal(
            barrier, inc=1, device_id={"wide": wide, "narrow": narrow}, device_id_type=pl.DeviceIdType.MESH
        )

    for k in range(1, NN):
        greet(w, (n + k) % NN)
    for k in range(1, NX):
        greet(wide_of(0, k), n)
    for k in range(1, NZ):
        greet(wide_of(k, 0), n)

    for target in range(NW):
        bundle[target % NX, target // NX, :, 0:VOC] = diff_ref[:, target * VOC : (target + 1) * VOC]
    relay[x] = bundle[x]

    values = h_ref[...].astype(f32)
    sq[n] = jnp.broadcast_to(jnp.sum(values * values, axis=1, keepdims=True), (REQ, 128))

    pl.semaphore_wait(barrier, NN + NX + NZ - 3)

    def sq_copy(k):
        return remote(sq.at[n], sq.at[n], sq_send.at[k], sq_recv.at[k], w, (n + k) % NN)

    def sq_arrival(k):
        peer = (n - k + NN) % NN
        return remote(sq.at[peer], sq.at[peer], sq_send.at[k], sq_recv.at[k], w, peer)

    for k in range(1, NN):
        sq_copy(k).start()

    def bundle_copy(k):
        return remote(bundle.at[(x + k) % NX], relay.at[x], b_send.at[k], b_recv.at[k], wide_of(0, k), n)

    def bundle_arrival(k):
        peer = (x - k + NX) % NX
        return remote(bundle.at[peer], relay.at[peer], b_send.at[k], b_recv.at[k], wide_of(0, k), n)

    def relay_copy(source, k):
        row = z * NX + source
        return remote(
            relay.at[source].at[(z + k) % NZ], recv_rows.at[row], a2a_send, a2a_recv, wide_of(k, 0), n
        )

    def relay_start(k):
        source = (x - k + NX) % NX
        recv_rows[z * NX + source] = relay[source, z]
        for far in FAR:
            relay_copy(source, far).start()

    for k in (2, 1, 3):
        bundle_copy(k).start()
    relay_start(0)

    live = lax.broadcasted_iota(jnp.int32, (CAP, NW), 0) < count_ref[pl.ds(n, 1), :]
    code = jnp.where(live, code_ref[n], 0)
    request = req_ref[n]
    spread = (
        lax.broadcasted_iota(jnp.int32, (NW, SLOTS), 1) // CAP == lax.broadcasted_iota(jnp.int32, (NW, SLOTS), 0)
    ).astype(bf16)
    picked = lax.broadcasted_iota(jnp.int32, (CAP, SLOTS), 1) % CAP == lax.broadcasted_iota(
        jnp.int32, (CAP, SLOTS), 0
    )

    def as_row(small):
        wide = jnp.dot(small.astype(f32).astype(bf16), spread, preferred_element_type=f32)
        return jnp.sum(jnp.where(picked, wide, 0.0), axis=0, keepdims=True)

    requests = as_row(request // 128) * 128.0 + as_row(request % 128)
    quarters = as_row(code) * 0.25

    for k in range(1, NN):
        sq_arrival(k).wait_recv()
    total = jnp.sum(sq[...], axis=0)[:, :1]
    scales = lax.rsqrt(total / D + EPS)
    act[w] = (values * scales * g_ref[...]).astype(bf16)

    top, bottom = pl.ds(0, REQ // 2), pl.ds(REQ // 2, REQ // 2)

    def z_copy(side, d, rows=None):
        step = 1 if side == 0 else -1
        block = act.at[wide_of(-step * d, 0)]
        block = block if rows is None else block.at[rows]
        return remote(block, block, z_send, z_recv.at[side, d + 1], wide_of(step, 0), n)

    def z_arrival(side, d, rows=None):
        step = 1 if side == 0 else -1
        block = act.at[wide_of(-step * d, 0)]
        block = block if rows is None else block.at[rows]
        return remote(block, block, z_send, z_recv.at[side, d], wide_of(step, 0), n)

    def x_copy(side, q, dz):
        step = 1 if side == 0 else -1
        block = act.at[wide_of(dz, 0)]
        return remote(block, block, x_send, x_recv.at[side, q], wide_of(0, step), n)

    def x_arrival(side, q, dz):
        step = 1 if side == 0 else -1
        block = act.at[wide_of(dz, -step)]
        return remote(block, block, x_send, x_recv.at[side, q], wide_of(0, step), n)

    def h_copy(side, q, dz):
        step = 1 if side == 0 else -1
        block = act.at[wide_of(dz, -step)].at[top if side == 0 else bottom]
        return remote(block, block, h_send, h_recv.at[side, q], wide_of(0, step), n)

    def h_arrival(side, q, dz):
        step = 1 if side == 0 else -1
        block = act.at[wide_of(dz, 2)].at[top if side == 0 else bottom]
        return remote(block, block, h_send, h_recv.at[side, q], wide_of(0, step), n)

    events = [[(0, 0)]] + [[(2 * d - 1, -d), (2 * d, d)] for d in range(1, 8)] + [[(15, 8)]]

    def forward_x(d):
        for q, dz in events[d]:
            for side in range(2):
                x_arrival(side, q, dz).wait_recv()
                h_copy(side, q, dz).start()

    def last_x(d):
        for q, dz in events[d]:
            for side in range(2):
                h_arrival(side, q, dz).wait_recv()

    def block_of(d):
        away = d // 2
        sign = 1 if d % 2 else -1
        return (z // 2 + jnp.where(z % 2 == 0, sign * away, -sign * away) + NN) % NN

    def product(d):
        block = block_of(d)
        left = act[pl.ds(block * (ROWS // REQ), ROWS // REQ)].reshape(ROWS, D // NN)
        part[block] = lax.dot_general(wt_ref[...], left, NT, preferred_element_type=f32)

    def add_rows(d):
        block = block_of(d)
        requested = lax.broadcasted_iota(jnp.int32, (ROWS, SLOTS), 0) + block * ROWS
        chosen = jnp.where(requests == requested.astype(f32), quarters, 0.0).astype(bf16)
        part[block] += lax.dot_general(rows_t[pl.ds(0, VOC)], chosen, NT, preferred_element_type=f32)

    for d in range(9):
        if d in range(1, 8):
            for side in range(2):
                z_arrival(side, d).wait_recv()
        if d == 8:
            z_arrival(0, 8, top).wait_recv()
            z_arrival(1, 8, bottom).wait_recv()
        if d < 7:
            for side in range(2):
                z_copy(side, d).start()
        if d == 7:
            z_copy(0, 7, top).start()
            z_copy(1, 7, bottom).start()
        for q, dz in events[d]:
            for side in range(2):
                x_copy(side, q, dz).start()
        if d < 3:
            k = (1, 3, 2)[d]
            bundle_arrival(k).wait_recv()
            relay_start(k)
        if d >= 1:
            forward_x(d - 1)
        if d >= 2:
            last_x(d - 2)
        if d >= 3:
            product(d - 2)
    forward_x(8)

    pltpu.make_async_copy(recv_rows.at[pl.ds(0, 60)], recv_rows.at[pl.ds(0, 60)], a2a_recv).wait()
    rows_t[...] = jnp.transpose(recv_rows[...].reshape(SLOTS, PADV))

    def north(k):
        return ((y + k + NY) % NY) * NC + c

    def away_of(block):
        return (block // NC - y + NY) % NY

    def pair_copy(block):
        r = away_of(block)
        return remote(part.at[block], pair.at[r], p_send.at[r], p_recv.at[r], w, y * NC + 1 - c)

    lanes = (pl.ds(0, ROWS // 2), pl.ds(ROWS // 2, ROWS // 2))

    def half_copy(side, block):
        step = 1 if side == 0 else -1
        return remote(part.at[block].at[:, lanes[side]], half.at[side], y_send.at[side], y_recv.at[side], w, north(step))

    def full_copy(side, block):
        step = 1 if side == 0 else -1
        return remote(part.at[block], full.at[side], y_send.at[2 + side], y_recv.at[2 + side], w, north(step))

    def across_cores(d):
        block = block_of(d)

        @pl.when(block % NC != c)
        def _():
            pair_copy(block).start()

    def from_core(d):
        block = block_of(d)
        r = away_of(block)

        @pl.when(block % NC == c)
        def _():
            pair_copy(block).wait_recv()
            part[block] += pair[r]

        @pl.when((block % NC == c) & (r == 2))
        def _():
            half_copy(0, block).start()
            half_copy(1, block).start()

    def to_owner(d):
        block = block_of(d)
        r = away_of(block)
        for side in range(2):

            @pl.when((block % NC == c) & (r == (1, 3)[side]))
            def _():
                half_copy(side, block).wait_recv()
                part[block, :, lanes[side]] += half[side]
                full_copy(side, block).start()

    for d in range(1, 17):
        if d in (7, 8):
            last_x(d)
            product(d)
        if d <= 8:
            add_rows(d)
            across_cores(d)
        if 1 <= d - 3 <= 8:
            from_core(d - 3)
        if 1 <= d - 8 <= 8:
            to_owner(d - 8)
    for side in range(2):
        full_copy(side, n).wait_recv()
    logits = part[n] + full[0] + full[1]

    def merged(buffer):
        peaks, masses = buffer[:, 0:1, :], buffer[:, 4:5, :]
        peak = jnp.max(peaks, axis=0)
        return peak, jnp.sum(masses * jnp.exp(peaks - peak[None]), axis=0)

    def put(buffer, index, peak, mass):
        buffer[index, 0:4, :] = jnp.broadcast_to(peak, (4, ROWS))
        buffer[index, 4:8, :] = jnp.broadcast_to(mass, (4, ROWS))

    peak = jnp.max(logits, axis=0, keepdims=True)
    mass = jnp.sum(jnp.exp(logits - peak), axis=0, keepdims=True)
    put(peaks_x, x, peak, mass)

    def sx_copy(k):
        return remote(peaks_x.at[x], peaks_x.at[x], sx_send.at[k], sx_recv.at[k], wide_of(0, k), n)

    for k in range(1, NX):
        sx_copy(k).start()
    for k in range(1, NX):
        sx_copy(k).wait_recv()
    peak, mass = merged(peaks_x)
    put(peaks_z, z, peak, mass)

    def sz_copy(k):
        return remote(peaks_z.at[z], peaks_z.at[z], sz_send.at[k], sz_recv.at[k], wide_of(k, 0), n)

    for k in FAR:
        sz_copy(k).start()
    for k in range(1, NZ):
        sz_copy(k).wait_recv()
    peak, mass = merged(peaks_z)
    o_ref[...] = logits - (peak + jnp.log(mass))

    for k in range(1, NN):
        sq_copy(k).wait_send()
    for k in range(1, NX):
        bundle_copy(k).wait_send()
    pltpu.make_async_copy(recv_rows.at[pl.ds(0, 60)], recv_rows.at[pl.ds(0, 60)], a2a_send).wait()
    pltpu.make_async_copy(act.at[pl.ds(0, 15)], act.at[pl.ds(0, 15)], z_send).wait()
    pltpu.make_async_copy(act.at[pl.ds(0, 32)], act.at[pl.ds(0, 32)], x_send).wait()
    pltpu.make_async_copy(act.at[pl.ds(0, 16)], act.at[pl.ds(0, 16)], h_send).wait()
    for r in range(NY):
        pair_copy(((y + r) % NY) * NC + 1 - c).wait_send()
    for side in range(2):
        half_copy(side, n).wait_send()
        full_copy(side, n).wait_send()
    for k in range(1, NX):
        sx_copy(k).wait_send()
    for k in range(1, NZ):
        sz_copy(k).wait_send()


def body(hidden, norm_gain, head_weight, diff_rows, slot_request, slot_code, slot_count):
    dma = pltpu.SemaphoreType.DMA
    vmem = pl.BlockSpec(memory_space=pltpu.VMEM)
    out = pl.pallas_call(
        head_kernel,
        name="head",
        out_shape=jax.ShapeDtypeStruct((VOC, ROWS), f32),
        in_specs=[vmem] * 7,
        out_specs=vmem,
        scratch_shapes=[
            pltpu.VMEM((NW, REQ, D // NN), bf16),
            pltpu.VMEM((NX, NZ, CAP, PADV), bf16),
            pltpu.VMEM((NX, NZ, CAP, PADV), bf16),
            pltpu.VMEM((NW, CAP, PADV), bf16),
            pltpu.VMEM((PADV, SLOTS), bf16),
            pltpu.VMEM((NN, VOC, ROWS), f32),
            pltpu.VMEM((NY, VOC, ROWS), f32),
            pltpu.VMEM((2, VOC, ROWS // 2), f32),
            pltpu.VMEM((2, VOC, ROWS), f32),
            pltpu.VMEM((NN, REQ, 128), f32),
            pltpu.VMEM((NX, 8, ROWS), f32),
            pltpu.VMEM((NZ, 8, ROWS), f32),
            dma((NN,)), dma((NN,)), dma((NX,)), dma((NX,)), dma, dma, dma, dma((2, 9)), dma, dma((2, 16)), dma, dma((2, 16)),
            dma((NY,)), dma((NY,)), dma((4,)), dma((4,)), dma((NX,)), dma((NX,)), dma((NZ,)), dma((NZ,)),
        ],
        compiler_params=pltpu.CompilerParams(has_side_effects=True, collective_id=0, vmem_limit_bytes=40 << 20),
    )(
        hidden,
        norm_gain[None, :],
        head_weight.T,
        diff_rows[0, 0],
        jnp.transpose(slot_request, (1, 2, 0)),
        jnp.transpose(slot_code, (1, 2, 0)),
        slot_count.T,
    )
    return out.T


def solution(mesh):
    placed = (
        P("wide", "narrow"),
        P("narrow"),
        P("narrow", "wide"),
        P("wide", "narrow", None, None),
        P(),
        P(),
        P(),
    )
    return jax.shard_map(
        body, mesh=mesh, in_specs=placed, out_specs=P("narrow", "wide"), check_vma=False
    )
```

```python
import functools

import jax
import jax.numpy as jnp
from jax import lax
from jax.experimental import pallas as pl
from jax.experimental.pallas import tpu as pltpu
from jax.sharding import PartitionSpec as P

D = 8192
EPS = 1e-05
NZ, NX, NY, NC = 16, 4, 4, 2
NW, NN = NZ * NX, NY * NC
REQ = 32
ROWS = 256
VOC = 500
PADV = 512
CAP = 8
SLOTS = NW * CAP
FAR = (8, 7, 9, 6, 10, 5, 11, 4, 12, 3, 13, 2, 14, 1, 15)

f32 = jnp.float32
bf16 = jnp.bfloat16
NT = (((1,), (1,)), ((), ()))


def remote(src, dst, send, recv, wide, narrow):
    return pltpu.make_async_remote_copy(
        src_ref=src,
        dst_ref=dst,
        send_sem=send,
        recv_sem=recv,
        device_id={"wide": wide, "narrow": narrow},
        device_id_type=pl.DeviceIdType.MESH,
    )


def head_kernel(
    h_ref, g_ref, wt_ref, diff_ref, req_ref, code_ref, count_ref, o_ref,
    act, bundle, relay, recv_rows, rows_t, part, pair, half, full, sq, peaks_x, peaks_z,
    sq_send, sq_recv, b_send, b_recv, a2a_send, a2a_recv, z_send, z_recv, x_send, x_recv, h_send, h_recv,
    p_send, p_recv, y_send, y_recv, sx_send, sx_recv, sz_send, sz_recv,
):
    w = lax.axis_index("wide")
    n = lax.axis_index("narrow")
    z, x, y, c = w // NX, w % NX, n // NC, n % NC

    def wide_of(dz, dx):
        return ((z + dz + NZ) % NZ) * NX + (x + dx + NX) % NX

    barrier = pltpu.get_barrier_semaphore()

    def greet(wide, narrow):
        pl.semaphore_signal(
            barrier, inc=1, device_id={"wide": wide, "narrow": narrow}, device_id_type=pl.DeviceIdType.MESH
        )

    for k in range(1, NN):
        greet(w, (n + k) % NN)
    for k in range(1, NX):
        greet(wide_of(0, k), n)
    for k in range(1, NZ):
        greet(wide_of(k, 0), n)

    for target in range(NW):
        bundle[target % NX, target // NX, :, 0:VOC] = diff_ref[:, target * VOC : (target + 1) * VOC]
    relay[x] = bundle[x]

    values = h_ref[...].astype(f32)
    diagonal = lax.broadcasted_iota(jnp.int32, (REQ, 128), 0) == lax.broadcasted_iota(jnp.int32, (REQ, 128), 1)
    squares = jnp.broadcast_to(jnp.sum(values * values, axis=1, keepdims=True), (REQ, 128))
    sq[n] = jnp.sum(jnp.where(diagonal, squares, 0.0), axis=0, keepdims=True)

    pl.semaphore_wait(barrier, NN + NX + NZ - 3)

    def sq_copy(k):
        return remote(sq.at[n], sq.at[n], sq_send.at[k], sq_recv.at[k], w, (n + k) % NN)

    def sq_arrival(k):
        peer = (n - k + NN) % NN
        return remote(sq.at[peer], sq.at[peer], sq_send.at[k], sq_recv.at[k], w, peer)

    for k in range(1, NN):
        sq_copy(k).start()

    def bundle_copy(k):
        return remote(bundle.at[(x + k) % NX], relay.at[x], b_send.at[k], b_recv.at[k], wide_of(0, k), n)

    def bundle_arrival(k):
        peer = (x - k + NX) % NX
        return remote(bundle.at[peer], relay.at[peer], b_send.at[k], b_recv.at[k], wide_of(0, k), n)

    def relay_copy(source, k):
        row = z * NX + source
        return remote(
            relay.at[source].at[(z + k) % NZ], recv_rows.at[row], a2a_send, a2a_recv, wide_of(k, 0), n
        )

    def relay_start(k, first=0, last=NZ - 1):
        source = (x - k + NX) % NX
        if first == 0:
            recv_rows[z * NX + source] = relay[source, z]
        for far in FAR[first:last]:
            relay_copy(source, far).start()

    for k in (2, 1, 3):
        bundle_copy(k).start()
    relay_start(0)

    live = lax.broadcasted_iota(jnp.int32, (CAP, NW), 0) < count_ref[pl.ds(n, 1), :]
    code = jnp.where(live, code_ref[n], 0)
    request = req_ref[n]
    spread = (
        lax.broadcasted_iota(jnp.int32, (NW, SLOTS), 1) // CAP == lax.broadcasted_iota(jnp.int32, (NW, SLOTS), 0)
    ).astype(bf16)
    picked = lax.broadcasted_iota(jnp.int32, (CAP, SLOTS), 1) % CAP == lax.broadcasted_iota(
        jnp.int32, (CAP, SLOTS), 0
    )

    def as_row(small):
        wide = jnp.dot(small.astype(f32).astype(bf16), spread, preferred_element_type=f32)
        return jnp.sum(jnp.where(picked, wide, 0.0), axis=0, keepdims=True)

    requests = as_row(request // 128) * 128.0 + as_row(request % 128)
    quarters = as_row(code) * 0.25

    for k in range(1, NN):
        sq_arrival(k).wait_recv()
    total = jnp.broadcast_to(jnp.sum(sq[...], axis=0), (REQ, 128))
    total = jnp.sum(jnp.where(diagonal, total, 0.0), axis=1, keepdims=True)
    scales = lax.rsqrt(total / D + EPS)
    act[w] = (values * scales * g_ref[...]).astype(bf16)

    top, bottom = pl.ds(0, REQ // 2), pl.ds(REQ // 2, REQ // 2)

    def z_copy(side, d, rows=None):
        step = 1 if side == 0 else -1
        block = act.at[wide_of(-step * d, 0)]
        block = block if rows is None else block.at[rows]
        return remote(block, block, z_send, z_recv.at[side, d + 1], wide_of(step, 0), n)

    def z_arrival(side, d, rows=None):
        step = 1 if side == 0 else -1
        block = act.at[wide_of(-step * d, 0)]
        block = block if rows is None else block.at[rows]
        return remote(block, block, z_send, z_recv.at[side, d], wide_of(step, 0), n)

    def x_copy(side, q, dz):
        step = 1 if side == 0 else -1
        block = act.at[wide_of(dz, 0)]
        return remote(block, block, x_send, x_recv.at[side, q], wide_of(0, step), n)

    def x_arrival(side, q, dz):
        step = 1 if side == 0 else -1
        block = act.at[wide_of(dz, -step)]
        return remote(block, block, x_send, x_recv.at[side, q], wide_of(0, step), n)

    def h_copy(side, q, dz):
        step = 1 if side == 0 else -1
        block = act.at[wide_of(dz, -step)].at[top if side == 0 else bottom]
        return remote(block, block, h_send, h_recv.at[side, q], wide_of(0, step), n)

    def h_arrival(side, q, dz):
        step = 1 if side == 0 else -1
        block = act.at[wide_of(dz, 2)].at[top if side == 0 else bottom]
        return remote(block, block, h_send, h_recv.at[side, q], wide_of(0, step), n)

    events = [[(0, 0)]] + [[(2 * d - 1, -d), (2 * d, d)] for d in range(1, 8)] + [[(15, 8)]]

    def forward_x(d):
        for q, dz in events[d]:
            for side in range(2):
                x_arrival(side, q, dz).wait_recv()
                h_copy(side, q, dz).start()

    def last_x(d):
        for q, dz in events[d]:
            for side in range(2):
                h_arrival(side, q, dz).wait_recv()

    def block_of(d):
        away = d // 2
        sign = 1 if d % 2 else -1
        return (z // 2 + jnp.where(z % 2 == 0, sign * away, -sign * away) + NN) % NN

    def product(d):
        block = block_of(d)
        left = act[pl.ds(block * (ROWS // REQ), ROWS // REQ)].reshape(ROWS, D // NN)
        part[block] = lax.dot_general(wt_ref[...], left, NT, preferred_element_type=f32)

    def add_rows(d):
        block = block_of(d)
        requested = lax.broadcasted_iota(jnp.int32, (ROWS, SLOTS), 0) + block * ROWS
        chosen = jnp.where(requests == requested.astype(f32), quarters, 0.0).astype(bf16)
        part[block] += lax.dot_general(rows_t[pl.ds(0, VOC)], chosen, NT, preferred_element_type=f32)

    def take_rows():
        pltpu.make_async_copy(recv_rows.at[pl.ds(0, 60)], recv_rows.at[pl.ds(0, 60)], a2a_recv).wait()
        rows_t[...] = jnp.transpose(recv_rows[...].reshape(SLOTS, PADV))

    def north(k):
        return ((y + k + NY) % NY) * NC + c

    def away_of(block):
        return (block // NC - y + NY) % NY

    def pair_copy(block):
        r = away_of(block)
        return remote(part.at[block], pair.at[r], p_send.at[r], p_recv.at[r], w, y * NC + 1 - c)

    lanes = (pl.ds(0, ROWS // 2), pl.ds(ROWS // 2, ROWS // 2))

    def half_copy(side, block):
        step = 1 if side == 0 else -1
        return remote(part.at[block].at[:, lanes[side]], half.at[side], y_send.at[side], y_recv.at[side], w, north(step))

    def full_copy(side, block):
        step = 1 if side == 0 else -1
        return remote(part.at[block], full.at[side], y_send.at[2 + side], y_recv.at[2 + side], w, north(step))

    def across_cores(d):
        block = block_of(d)

        @pl.when(block % NC != c)
        def _():
            pair_copy(block).start()

    def from_core(d):
        block = block_of(d)
        r = away_of(block)

        @pl.when(block % NC == c)
        def _():
            pair_copy(block).wait_recv()
            part[block] += pair[r]

        @pl.when((block % NC == c) & (r == 2))
        def _():
            half_copy(0, block).start()
            half_copy(1, block).start()

    def to_owner(d):
        block = block_of(d)
        r = away_of(block)
        for side in range(2):

            @pl.when((block % NC == c) & (r == (1, 3)[side]))
            def _():
                half_copy(side, block).wait_recv()
                part[block, :, lanes[side]] += half[side]
                full_copy(side, block).start()

    for d in range(9):
        if d in range(1, 8):
            for side in range(2):
                z_arrival(side, d).wait_recv()
        if d == 8:
            z_arrival(0, 8, top).wait_recv()
            z_arrival(1, 8, bottom).wait_recv()
        if d < 7:
            for side in range(2):
                z_copy(side, d).start()
        if d == 7:
            z_copy(0, 7, top).start()
            z_copy(1, 7, bottom).start()
        for q, dz in events[d]:
            for side in range(2):
                x_copy(side, q, dz).start()
        if d == 0:
            bundle_arrival(1).wait_recv()
            relay_start(1, 0, 8)
        if d == 1:
            relay_start(1, 8, 15)
        if d == 2:
            bundle_arrival(3).wait_recv()
            relay_start(3, 0, 8)
        if d == 3:
            relay_start(3, 8, 15)
        if d == 4:
            bundle_arrival(2).wait_recv()
            relay_start(2, 0, 8)
        if d == 5:
            relay_start(2, 8, 15)
        if d >= 1:
            forward_x(d - 1)
        if d >= 2:
            last_x(d - 2)
        if d >= 3:
            product(d - 2)
        if d == 7:
            take_rows()
    forward_x(8)
    add_rows(1)
    across_cores(1)
    add_rows(2)
    across_cores(2)
    add_rows(3)
    across_cores(3)
    add_rows(4)
    across_cores(4)
    add_rows(5)
    across_cores(5)
    add_rows(6)
    across_cores(6)
    from_core(1)
    from_core(2)
    from_core(3)
    from_core(4)
    from_core(5)
    from_core(6)
    last_x(7)
    product(7)
    add_rows(7)
    across_cores(7)
    last_x(8)
    product(8)
    add_rows(8)
    across_cores(8)
    from_core(7)
    from_core(8)
    to_owner(1)
    to_owner(2)
    to_owner(3)
    to_owner(4)
    to_owner(5)
    to_owner(6)
    to_owner(7)
    to_owner(8)

    for side in range(2):
        full_copy(side, n).wait_recv()
    logits = part[n] + full[0] + full[1]

    def merged(buffer):
        peaks, masses = buffer[:, 0:1, :], buffer[:, 1:2, :]
        peak = jnp.max(peaks, axis=0)
        return peak, jnp.sum(masses * jnp.exp(peaks - peak[None]), axis=0)

    def put(buffer, index, peak, mass):
        buffer[index, 0:1, :] = peak
        buffer[index, 1:2, :] = mass

    peak = jnp.max(logits, axis=0, keepdims=True)
    mass = jnp.sum(jnp.exp(logits - peak), axis=0, keepdims=True)
    put(peaks_x, x, peak, mass)

    def sx_copy(k):
        return remote(peaks_x.at[x], peaks_x.at[x], sx_send.at[k], sx_recv.at[k], wide_of(0, k), n)

    for k in range(1, NX):
        sx_copy(k).start()
    for k in range(1, NX):
        sx_copy(k).wait_recv()
    peak, mass = merged(peaks_x)
    put(peaks_z, z, peak, mass)

    def sz_copy(k):
        return remote(peaks_z.at[z], peaks_z.at[z], sz_send.at[k], sz_recv.at[k], wide_of(k, 0), n)

    for k in FAR:
        sz_copy(k).start()
    for k in range(1, NZ):
        sz_copy(k).wait_recv()
    peak, mass = merged(peaks_z)
    o_ref[...] = logits - (peak + jnp.log(mass))

    for k in range(1, NN):
        sq_copy(k).wait_send()
    for k in range(1, NX):
        bundle_copy(k).wait_send()
    pltpu.make_async_copy(recv_rows.at[pl.ds(0, 60)], recv_rows.at[pl.ds(0, 60)], a2a_send).wait()
    pltpu.make_async_copy(act.at[pl.ds(0, 15)], act.at[pl.ds(0, 15)], z_send).wait()
    pltpu.make_async_copy(act.at[pl.ds(0, 32)], act.at[pl.ds(0, 32)], x_send).wait()
    pltpu.make_async_copy(act.at[pl.ds(0, 16)], act.at[pl.ds(0, 16)], h_send).wait()
    for r in range(NY):
        pair_copy(((y + r) % NY) * NC + 1 - c).wait_send()
    for side in range(2):
        half_copy(side, n).wait_send()
        full_copy(side, n).wait_send()
    for k in range(1, NX):
        sx_copy(k).wait_send()
    for k in range(1, NZ):
        sz_copy(k).wait_send()


def body(hidden, norm_gain, head_weight, diff_rows, slot_request, slot_code, slot_count):
    dma = pltpu.SemaphoreType.DMA
    vmem = pl.BlockSpec(memory_space=pltpu.VMEM)
    out = pl.pallas_call(
        head_kernel,
        name="head",
        out_shape=jax.ShapeDtypeStruct((VOC, ROWS), f32),
        in_specs=[vmem] * 7,
        out_specs=vmem,
        scratch_shapes=[
            pltpu.VMEM((NW, REQ, D // NN), bf16),
            pltpu.VMEM((NX, NZ, CAP, PADV), bf16),
            pltpu.VMEM((NX, NZ, CAP, PADV), bf16),
            pltpu.VMEM((NW, CAP, PADV), bf16),
            pltpu.VMEM((PADV, SLOTS), bf16),
            pltpu.VMEM((NN, VOC, ROWS), f32),
            pltpu.VMEM((NY, VOC, ROWS), f32),
            pltpu.VMEM((2, VOC, ROWS // 2), f32),
            pltpu.VMEM((2, VOC, ROWS), f32),
            pltpu.VMEM((NN, 1, 128), f32),
            pltpu.VMEM((NX, 2, ROWS), f32),
            pltpu.VMEM((NZ, 2, ROWS), f32),
            dma((NN,)), dma((NN,)), dma((NX,)), dma((NX,)), dma, dma, dma, dma((2, 9)), dma, dma((2, 16)), dma, dma((2, 16)),
            dma((NY,)), dma((NY,)), dma((4,)), dma((4,)), dma((NX,)), dma((NX,)), dma((NZ,)), dma((NZ,)),
        ],
        compiler_params=pltpu.CompilerParams(has_side_effects=True, collective_id=0, vmem_limit_bytes=40 << 20),
    )(
        hidden,
        norm_gain[None, :],
        head_weight.T,
        diff_rows[0, 0],
        jnp.transpose(slot_request, (1, 2, 0)),
        jnp.transpose(slot_code, (1, 2, 0)),
        slot_count.T,
    )
    return out.T


def solution(mesh):
    placed = (
        P("wide", "narrow"),
        P("narrow"),
        P("narrow", "wide"),
        P("wide", "narrow", None, None),
        P(),
        P(),
        P(),
    )
    return jax.shard_map(
        body, mesh=mesh, in_specs=placed, out_specs=P("narrow", "wide"), check_vma=False
    )
```

```python
import functools

import jax
import jax.numpy as jnp
from jax import lax
from jax.experimental import pallas as pl
from jax.experimental.pallas import tpu as pltpu
from jax.sharding import PartitionSpec as P

D = 8192
EPS = 1e-05
NZ, NX, NY, NC = 16, 4, 4, 2
NW, NN = NZ * NX, NY * NC
REQ = 32
ROWS = 256
VOC = 500
PADV = 512
CAP = 8
SLOTS = NW * CAP
FAR = (8, 7, 9, 6, 10, 5, 11, 4, 12, 3, 13, 2, 14, 1, 15)

f32 = jnp.float32
bf16 = jnp.bfloat16
NT = (((1,), (1,)), ((), ()))


def remote(src, dst, send, recv, wide, narrow):
    return pltpu.make_async_remote_copy(
        src_ref=src,
        dst_ref=dst,
        send_sem=send,
        recv_sem=recv,
        device_id={"wide": wide, "narrow": narrow},
        device_id_type=pl.DeviceIdType.MESH,
    )


def head_kernel(
    h_ref, g_ref, wt_ref, diff_ref, req_ref, code_ref, count_ref, o_ref,
    act, bundle, relay, recv_rows, rows_t, part, pair, half, full, sq, peaks_x, peaks_z,
    sq_send, sq_recv, b_send, b_recv, a2a_send, a2a_recv, z_send, z_recv, x_send, x_recv, h_send, h_recv,
    p_send, p_recv, y_send, y_recv, sx_send, sx_recv, sz_send, sz_recv,
):
    w = lax.axis_index("wide")
    n = lax.axis_index("narrow")
    z, x, y, c = w // NX, w % NX, n // NC, n % NC

    def wide_of(dz, dx):
        return ((z + dz + NZ) % NZ) * NX + (x + dx + NX) % NX

    barrier = pltpu.get_barrier_semaphore()

    def greet(wide, narrow):
        pl.semaphore_signal(
            barrier, inc=1, device_id={"wide": wide, "narrow": narrow}, device_id_type=pl.DeviceIdType.MESH
        )

    for k in range(1, NN):
        greet(w, (n + k) % NN)
    for k in range(1, NX):
        greet(wide_of(0, k), n)
    for k in range(1, NZ):
        greet(wide_of(k, 0), n)

    for target in range(NW):
        bundle[target % NX, target // NX, :, 0:VOC] = diff_ref[:, target * VOC : (target + 1) * VOC]
    relay[x] = bundle[x]

    values = h_ref[...].astype(f32)
    diagonal = lax.broadcasted_iota(jnp.int32, (REQ, 128), 0) == lax.broadcasted_iota(jnp.int32, (REQ, 128), 1)
    squares = jnp.broadcast_to(jnp.sum(values * values, axis=1, keepdims=True), (REQ, 128))
    sq[n] = jnp.sum(jnp.where(diagonal, squares, 0.0), axis=0, keepdims=True)

    pl.semaphore_wait(barrier, NN + NX + NZ - 3)

    def sq_copy(k):
        return remote(sq.at[n], sq.at[n], sq_send.at[k], sq_recv.at[k], w, (n + k) % NN)

    def sq_arrival(k):
        peer = (n - k + NN) % NN
        return remote(sq.at[peer], sq.at[peer], sq_send.at[k], sq_recv.at[k], w, peer)

    for k in range(1, NN):
        sq_copy(k).start()

    def bundle_copy(k):
        return remote(bundle.at[(x + k) % NX], relay.at[x], b_send.at[k], b_recv.at[k], wide_of(0, k), n)

    def bundle_arrival(k):
        peer = (x - k + NX) % NX
        return remote(bundle.at[peer], relay.at[peer], b_send.at[k], b_recv.at[k], wide_of(0, k), n)

    def relay_copy(source, k):
        row = z * NX + source
        return remote(
            relay.at[source].at[(z + k) % NZ], recv_rows.at[row], a2a_send, a2a_recv, wide_of(k, 0), n
        )

    def relay_start(k, first=0, last=NZ - 1):
        source = (x - k + NX) % NX
        if first == 0:
            recv_rows[z * NX + source] = relay[source, z]
        for far in FAR[first:last]:
            relay_copy(source, far).start()

    for k in (2, 1, 3):
        bundle_copy(k).start()
    relay_start(0)

    live = lax.broadcasted_iota(jnp.int32, (CAP, NW), 0) < count_ref[pl.ds(n, 1), :]
    code = jnp.where(live, code_ref[n], 0)
    request = req_ref[n]
    spread = (
        lax.broadcasted_iota(jnp.int32, (NW, SLOTS), 1) // CAP == lax.broadcasted_iota(jnp.int32, (NW, SLOTS), 0)
    ).astype(bf16)
    picked = lax.broadcasted_iota(jnp.int32, (CAP, SLOTS), 1) % CAP == lax.broadcasted_iota(
        jnp.int32, (CAP, SLOTS), 0
    )

    def as_row(small):
        wide = jnp.dot(small.astype(f32).astype(bf16), spread, preferred_element_type=f32)
        return jnp.sum(jnp.where(picked, wide, 0.0), axis=0, keepdims=True)

    requests = as_row(request // 128) * 128.0 + as_row(request % 128)
    quarters = as_row(code) * 0.25

    for k in range(1, NN):
        sq_arrival(k).wait_recv()
    total = jnp.broadcast_to(jnp.sum(sq[...], axis=0), (REQ, 128))
    total = jnp.sum(jnp.where(diagonal, total, 0.0), axis=1, keepdims=True)
    scales = lax.rsqrt(total / D + EPS)
    act[w] = (values * scales * g_ref[...]).astype(bf16)

    top, bottom = pl.ds(0, REQ // 2), pl.ds(REQ // 2, REQ // 2)

    def z_copy(side, d, rows=None):
        step = 1 if side == 0 else -1
        block = act.at[wide_of(-step * d, 0)]
        block = block if rows is None else block.at[rows]
        return remote(block, block, z_send, z_recv.at[side, d + 1], wide_of(step, 0), n)

    def z_arrival(side, d, rows=None):
        step = 1 if side == 0 else -1
        block = act.at[wide_of(-step * d, 0)]
        block = block if rows is None else block.at[rows]
        return remote(block, block, z_send, z_recv.at[side, d], wide_of(step, 0), n)

    def x_copy(side, q, dz):
        step = 1 if side == 0 else -1
        block = act.at[wide_of(dz, 0)]
        return remote(block, block, x_send, x_recv.at[side, q], wide_of(0, step), n)

    def x_arrival(side, q, dz):
        step = 1 if side == 0 else -1
        block = act.at[wide_of(dz, -step)]
        return remote(block, block, x_send, x_recv.at[side, q], wide_of(0, step), n)

    def h_copy(side, q, dz):
        step = 1 if side == 0 else -1
        block = act.at[wide_of(dz, -step)].at[top if side == 0 else bottom]
        return remote(block, block, h_send, h_recv.at[side, q], wide_of(0, step), n)

    def h_arrival(side, q, dz):
        step = 1 if side == 0 else -1
        block = act.at[wide_of(dz, 2)].at[top if side == 0 else bottom]
        return remote(block, block, h_send, h_recv.at[side, q], wide_of(0, step), n)

    events = [[(0, 0)]] + [[(2 * d - 1, -d), (2 * d, d)] for d in range(1, 8)] + [[(15, 8)]]

    def forward_x(d):
        for q, dz in events[d]:
            for side in range(2):
                x_arrival(side, q, dz).wait_recv()
                h_copy(side, q, dz).start()

    def last_x(d):
        for q, dz in events[d]:
            for side in range(2):
                h_arrival(side, q, dz).wait_recv()

    def block_of(d):
        away = d // 2
        sign = 1 if d % 2 else -1
        return (z // 2 + jnp.where(z % 2 == 0, sign * away, -sign * away) + NN) % NN

    def product(d):
        block = block_of(d)
        left = act[pl.ds(block * (ROWS // REQ), ROWS // REQ)].reshape(ROWS, D // NN)
        part[block] = lax.dot_general(wt_ref[...], left, NT, preferred_element_type=f32)

    def add_rows(d):
        block = block_of(d)
        requested = lax.broadcasted_iota(jnp.int32, (ROWS, SLOTS), 0) + block * ROWS
        chosen = jnp.where(requests == requested.astype(f32), quarters, 0.0).astype(bf16)
        part[block] += lax.dot_general(rows_t[pl.ds(0, VOC)], chosen, NT, preferred_element_type=f32)

    def take_rows():
        pltpu.make_async_copy(recv_rows.at[pl.ds(0, 60)], recv_rows.at[pl.ds(0, 60)], a2a_recv).wait()
        rows_t[...] = jnp.transpose(recv_rows[...].reshape(SLOTS, PADV))

    def north(k):
        return ((y + k + NY) % NY) * NC + c

    def away_of(block):
        return (block // NC - y + NY) % NY

    def pair_copy(block):
        r = away_of(block)
        return remote(part.at[block], pair.at[r], p_send.at[r], p_recv.at[r], w, y * NC + 1 - c)

    lanes = (pl.ds(0, ROWS // 2), pl.ds(ROWS // 2, ROWS // 2))

    def half_copy(side, block):
        step = 1 if side == 0 else -1
        return remote(part.at[block].at[:, lanes[side]], half.at[side], y_send.at[side], y_recv.at[side], w, north(step))

    def full_copy(side, block):
        step = 1 if side == 0 else -1
        return remote(part.at[block], full.at[side], y_send.at[2 + side], y_recv.at[2 + side], w, north(step))

    def across_cores(d):
        block = block_of(d)

        @pl.when(block % NC != c)
        def _():
            pair_copy(block).start()

    def from_core(d):
        block = block_of(d)
        r = away_of(block)

        @pl.when(block % NC == c)
        def _():
            pair_copy(block).wait_recv()
            part[block] += pair[r]

        @pl.when((block % NC == c) & (r == 2))
        def _():
            half_copy(0, block).start()
            half_copy(1, block).start()

    def to_owner(d):
        block = block_of(d)
        r = away_of(block)
        for side in range(2):

            @pl.when((block % NC == c) & (r == (1, 3)[side]))
            def _():
                half_copy(side, block).wait_recv()
                part[block, :, lanes[side]] += half[side]
                full_copy(side, block).start()

    for d in range(9):
        for side in range(2 if d < 7 else 0):
            if d > 0:
                z_arrival(side, d).wait_recv()
            z_copy(side, d).start()
            if d > 0:
                q, dz = events[d][side]
                x_copy(0, q, dz).start()
                x_copy(1, q, dz).start()
        if d == 7:
            for side in range(2):
                z_arrival(side, d).wait_recv()
        if d == 8:
            z_arrival(0, 8, top).wait_recv()
            z_arrival(1, 8, bottom).wait_recv()
        if d == 7:
            z_copy(0, 7, top).start()
            z_copy(1, 7, bottom).start()
        for q, dz in events[d] if d in (0, 7, 8) else ():
            for side in range(2):
                x_copy(side, q, dz).start()
        if d == 0:
            bundle_arrival(1).wait_recv()
            relay_start(1, 0, 5)
        if d == 1:
            relay_start(1, 5, 10)
        if d == 2:
            relay_start(1, 10, 15)
        if d == 3:
            bundle_arrival(3).wait_recv()
            relay_start(3, 0, 8)
        if d == 4:
            relay_start(3, 8, 15)
        if d == 5:
            bundle_arrival(2).wait_recv()
            relay_start(2, 0, 8)
        if d == 6:
            relay_start(2, 8, 15)
        if d >= 1:
            forward_x(d - 1)
        if d >= 2:
            last_x(d - 2)
        if d >= 3:
            product(d - 2)
        if d == 7:
            take_rows()
    forward_x(8)
    add_rows(1)
    across_cores(1)
    add_rows(2)
    across_cores(2)
    add_rows(3)
    across_cores(3)
    add_rows(4)
    across_cores(4)
    add_rows(5)
    across_cores(5)
    add_rows(6)
    across_cores(6)
    from_core(1)
    from_core(2)
    from_core(3)
    from_core(4)
    from_core(5)
    from_core(6)
    last_x(7)
    product(7)
    add_rows(7)
    across_cores(7)
    last_x(8)
    product(8)
    add_rows(8)
    across_cores(8)
    from_core(7)
    from_core(8)
    to_owner(1)
    to_owner(2)
    to_owner(3)
    to_owner(4)
    to_owner(5)
    to_owner(6)
    to_owner(7)
    to_owner(8)

    for side in range(2):
        full_copy(side, n).wait_recv()
    logits = part[n] + full[0] + full[1]

    def merged(buffer):
        peaks, masses = buffer[:, 0:1, :], buffer[:, 1:2, :]
        peak = jnp.max(peaks, axis=0)
        return peak, jnp.sum(masses * jnp.exp(peaks - peak[None]), axis=0)

    def put(buffer, index, peak, mass):
        buffer[index, 0:1, :] = peak
        buffer[index, 1:2, :] = mass

    peak = jnp.max(logits, axis=0, keepdims=True)
    mass = jnp.sum(jnp.exp(logits - peak), axis=0, keepdims=True)
    put(peaks_x, x, peak, mass)

    def sx_copy(k):
        return remote(peaks_x.at[x], peaks_x.at[x], sx_send.at[k], sx_recv.at[k], wide_of(0, k), n)

    for k in range(1, NX):
        sx_copy(k).start()
    for k in range(1, NX):
        sx_copy(k).wait_recv()
    peak, mass = merged(peaks_x)
    put(peaks_z, z, peak, mass)

    def sz_copy(k):
        return remote(peaks_z.at[z], peaks_z.at[z], sz_send.at[k], sz_recv.at[k], wide_of(k, 0), n)

    for k in FAR:
        sz_copy(k).start()
    for k in range(1, NZ):
        sz_copy(k).wait_recv()
    peak, mass = merged(peaks_z)
    o_ref[...] = logits - (peak + jnp.log(mass))

    for k in range(1, NN):
        sq_copy(k).wait_send()
    for k in range(1, NX):
        bundle_copy(k).wait_send()
    pltpu.make_async_copy(recv_rows.at[pl.ds(0, 60)], recv_rows.at[pl.ds(0, 60)], a2a_send).wait()
    pltpu.make_async_copy(act.at[pl.ds(0, 15)], act.at[pl.ds(0, 15)], z_send).wait()
    pltpu.make_async_copy(act.at[pl.ds(0, 32)], act.at[pl.ds(0, 32)], x_send).wait()
    pltpu.make_async_copy(act.at[pl.ds(0, 16)], act.at[pl.ds(0, 16)], h_send).wait()
    for r in range(NY):
        pair_copy(((y + r) % NY) * NC + 1 - c).wait_send()
    for side in range(2):
        half_copy(side, n).wait_send()
        full_copy(side, n).wait_send()
    for k in range(1, NX):
        sx_copy(k).wait_send()
    for k in range(1, NZ):
        sz_copy(k).wait_send()


def body(hidden, norm_gain, head_weight, diff_rows, slot_request, slot_code, slot_count):
    dma = pltpu.SemaphoreType.DMA
    vmem = pl.BlockSpec(memory_space=pltpu.VMEM)
    out = pl.pallas_call(
        head_kernel,
        name="head",
        out_shape=jax.ShapeDtypeStruct((VOC, ROWS), f32),
        in_specs=[vmem] * 7,
        out_specs=vmem,
        scratch_shapes=[
            pltpu.VMEM((NW, REQ, D // NN), bf16),
            pltpu.VMEM((NX, NZ, CAP, PADV), bf16),
            pltpu.VMEM((NX, NZ, CAP, PADV), bf16),
            pltpu.VMEM((NW, CAP, PADV), bf16),
            pltpu.VMEM((PADV, SLOTS), bf16),
            pltpu.VMEM((NN, VOC, ROWS), f32),
            pltpu.VMEM((NY, VOC, ROWS), f32),
            pltpu.VMEM((2, VOC, ROWS // 2), f32),
            pltpu.VMEM((2, VOC, ROWS), f32),
            pltpu.VMEM((NN, 1, 128), f32),
            pltpu.VMEM((NX, 2, ROWS), f32),
            pltpu.VMEM((NZ, 2, ROWS), f32),
            dma((NN,)), dma((NN,)), dma((NX,)), dma((NX,)), dma, dma, dma, dma((2, 9)), dma, dma((2, 16)), dma, dma((2, 16)),
            dma((NY,)), dma((NY,)), dma((4,)), dma((4,)), dma((NX,)), dma((NX,)), dma((NZ,)), dma((NZ,)),
        ],
        compiler_params=pltpu.CompilerParams(has_side_effects=True, collective_id=0, vmem_limit_bytes=40 << 20),
    )(
        hidden,
        norm_gain[None, :],
        head_weight.T,
        diff_rows[0, 0],
        jnp.transpose(slot_request, (1, 2, 0)),
        jnp.transpose(slot_code, (1, 2, 0)),
        slot_count.T,
    )
    return out.T


def solution(mesh):
    placed = (
        P("wide", "narrow"),
        P("narrow"),
        P("narrow", "wide"),
        P("wide", "narrow", None, None),
        P(),
        P(),
        P(),
    )
    return jax.shard_map(
        body, mesh=mesh, in_specs=placed, out_specs=P("narrow", "wide"), check_vma=False
    )
```

```python
import functools

import jax
import jax.numpy as jnp
from jax import lax
from jax.experimental import pallas as pl
from jax.experimental.pallas import tpu as pltpu
from jax.sharding import PartitionSpec as P

D = 8192
EPS = 1e-05
NZ, NX, NY, NC = 16, 4, 4, 2
NW, NN = NZ * NX, NY * NC
REQ = 32
ROWS = 256
VOC = 500
PADV = 512
CAP = 8
SLOTS = NW * CAP
FAR = (8, 7, 9, 6, 10, 5, 11, 4, 12, 3, 13, 2, 14, 1, 15)

f32 = jnp.float32
bf16 = jnp.bfloat16
NT = (((1,), (1,)), ((), ()))


def remote(src, dst, send, recv, wide, narrow):
    return pltpu.make_async_remote_copy(
        src_ref=src,
        dst_ref=dst,
        send_sem=send,
        recv_sem=recv,
        device_id={"wide": wide, "narrow": narrow},
        device_id_type=pl.DeviceIdType.MESH,
    )


def head_kernel(
    h_ref, g_ref, wt_ref, diff_ref, req_ref, code_ref, count_ref, o_ref,
    act, bundle, relay, recv_rows, rows_t, part, pair, half, full, sq, peaks_x, peaks_z,
    sq_send, sq_recv, b_send, b_recv, a2a_send, a2a_recv, z_send, z_recv, x_send, x_recv, h_send, h_recv,
    p_send, p_recv, y_send, y_recv, sx_send, sx_recv, sz_send, sz_recv,
):
    w = lax.axis_index("wide")
    n = lax.axis_index("narrow")
    z, x, y, c = w // NX, w % NX, n // NC, n % NC

    def wide_of(dz, dx):
        return ((z + dz + NZ) % NZ) * NX + (x + dx + NX) % NX

    barrier = pltpu.get_barrier_semaphore()

    def greet(wide, narrow):
        pl.semaphore_signal(
            barrier, inc=1, device_id={"wide": wide, "narrow": narrow}, device_id_type=pl.DeviceIdType.MESH
        )

    for k in FAR:
        greet(wide_of(k, 0), n)
    for k in (4, 5, 3, 2, 6, 1, 7):
        greet(w, (n + k) % NN)
    for k in (2, 1, 3):
        greet(wide_of(0, k), n)

    for target in range(NW):
        bundle[target % NX, target // NX, :, 0:VOC] = diff_ref[:, target * VOC : (target + 1) * VOC]
    relay[x] = bundle[x]

    values = h_ref[...].astype(f32)
    diagonal = lax.broadcasted_iota(jnp.int32, (REQ, 128), 0) == lax.broadcasted_iota(jnp.int32, (REQ, 128), 1)
    squares = jnp.broadcast_to(jnp.sum(values * values, axis=1, keepdims=True), (REQ, 128))
    sq[n] = jnp.sum(jnp.where(diagonal, squares, 0.0), axis=0, keepdims=True)

    pl.semaphore_wait(barrier, NN + NX + NZ - 3)

    def sq_copy(k):
        return remote(sq.at[n], sq.at[n], sq_send.at[k], sq_recv.at[k], w, (n + k) % NN)

    def sq_arrival(k):
        peer = (n - k + NN) % NN
        return remote(sq.at[peer], sq.at[peer], sq_send.at[k], sq_recv.at[k], w, peer)

    for k in (4, 5, 3, 2, 6, 1, 7):
        sq_copy(k).start()

    def bundle_copy(k):
        return remote(bundle.at[(x + k) % NX], relay.at[x], b_send.at[k], b_recv.at[k], wide_of(0, k), n)

    def bundle_arrival(k):
        peer = (x - k + NX) % NX
        return remote(bundle.at[peer], relay.at[peer], b_send.at[k], b_recv.at[k], wide_of(0, k), n)

    def relay_copy(source, k):
        row = z * NX + source
        return remote(
            relay.at[source].at[(z + k) % NZ], recv_rows.at[row], a2a_send, a2a_recv, wide_of(k, 0), n
        )

    def relay_start(k, first=0, last=NZ - 1):
        source = (x - k + NX) % NX
        if first == 0:
            recv_rows[z * NX + source] = relay[source, z]
        for far in FAR[first:last]:
            relay_copy(source, far).start()

    for k in (2, 1, 3):
        bundle_copy(k).start()
    relay_start(0)

    live = lax.broadcasted_iota(jnp.int32, (CAP, NW), 0) < count_ref[pl.ds(n, 1), :]
    code = jnp.where(live, code_ref[n], 0)
    request = req_ref[n]
    spread = (
        lax.broadcasted_iota(jnp.int32, (NW, SLOTS), 1) // CAP == lax.broadcasted_iota(jnp.int32, (NW, SLOTS), 0)
    ).astype(bf16)
    picked = lax.broadcasted_iota(jnp.int32, (CAP, SLOTS), 1) % CAP == lax.broadcasted_iota(
        jnp.int32, (CAP, SLOTS), 0
    )

    def as_row(small):
        wide = jnp.dot(small.astype(f32).astype(bf16), spread, preferred_element_type=f32)
        return jnp.sum(jnp.where(picked, wide, 0.0), axis=0, keepdims=True)

    requests = as_row(request // 128) * 128.0 + as_row(request % 128)
    quarters = as_row(code) * 0.25

    for k in range(1, NN):
        sq_arrival(k).wait_recv()
    total = jnp.broadcast_to(jnp.sum(sq[...], axis=0), (REQ, 128))
    total = jnp.sum(jnp.where(diagonal, total, 0.0), axis=1, keepdims=True)
    scales = lax.rsqrt(total / D + EPS)
    act[w] = (values * scales * g_ref[...]).astype(bf16)

    top, bottom = pl.ds(0, REQ // 2), pl.ds(REQ // 2, REQ // 2)

    def z_copy(side, d, rows=None):
        step = 1 if side == 0 else -1
        block = act.at[wide_of(-step * d, 0)]
        block = block if rows is None else block.at[rows]
        return remote(block, block, z_send, z_recv.at[side, d + 1], wide_of(step, 0), n)

    def z_arrival(side, d, rows=None):
        step = 1 if side == 0 else -1
        block = act.at[wide_of(-step * d, 0)]
        block = block if rows is None else block.at[rows]
        return remote(block, block, z_send, z_recv.at[side, d], wide_of(step, 0), n)

    def x_copy(side, q, dz):
        step = 1 if side == 0 else -1
        block = act.at[wide_of(dz, 0)]
        return remote(block, block, x_send, x_recv.at[side, q], wide_of(0, step), n)

    def x_arrival(side, q, dz):
        step = 1 if side == 0 else -1
        block = act.at[wide_of(dz, -step)]
        return remote(block, block, x_send, x_recv.at[side, q], wide_of(0, step), n)

    def h_copy(side, q, dz):
        step = 1 if side == 0 else -1
        block = act.at[wide_of(dz, -step)].at[top if side == 0 else bottom]
        return remote(block, block, h_send, h_recv.at[side, q], wide_of(0, step), n)

    def h_arrival(side, q, dz):
        step = 1 if side == 0 else -1
        block = act.at[wide_of(dz, 2)].at[top if side == 0 else bottom]
        return remote(block, block, h_send, h_recv.at[side, q], wide_of(0, step), n)

    events = [[(0, 0)]] + [[(2 * d - 1, -d), (2 * d, d)] for d in range(1, 8)] + [[(15, 8)]]

    def forward_x(d):
        for q, dz in events[d]:
            for side in range(2):
                x_arrival(side, q, dz).wait_recv()
                h_copy(side, q, dz).start()

    def last_x(d):
        for q, dz in events[d]:
            for side in range(2):
                h_arrival(side, q, dz).wait_recv()

    def block_of(d):
        away = d // 2
        sign = 1 if d % 2 else -1
        return (z // 2 + jnp.where(z % 2 == 0, sign * away, -sign * away) + NN) % NN

    def product(d):
        block = block_of(d)
        left = act[pl.ds(block * (ROWS // REQ), ROWS // REQ)].reshape(ROWS, D // NN)
        part[block] = lax.dot_general(wt_ref[...], left, NT, preferred_element_type=f32)

    def add_rows(d):
        block = block_of(d)
        requested = lax.broadcasted_iota(jnp.int32, (ROWS, SLOTS), 0) + block * ROWS
        chosen = jnp.where(requests == requested.astype(f32), quarters, 0.0).astype(bf16)
        part[block] += lax.dot_general(rows_t[pl.ds(0, VOC)], chosen, NT, preferred_element_type=f32)

    def take_rows():
        pltpu.make_async_copy(recv_rows.at[pl.ds(0, 60)], recv_rows.at[pl.ds(0, 60)], a2a_recv).wait()
        rows_t[...] = jnp.transpose(recv_rows[...].reshape(SLOTS, PADV))

    def north(k):
        return ((y + k + NY) % NY) * NC + c

    def away_of(block):
        return (block // NC - y + NY) % NY

    def pair_copy(block):
        r = away_of(block)
        return remote(part.at[block], pair.at[r], p_send.at[r], p_recv.at[r], w, y * NC + 1 - c)

    lanes = (pl.ds(0, ROWS // 2), pl.ds(ROWS // 2, ROWS // 2))

    def half_copy(side, block):
        step = 1 if side == 0 else -1
        return remote(part.at[block].at[:, lanes[side]], half.at[side], y_send.at[side], y_recv.at[side], w, north(step))

    def full_copy(side, block):
        step = 1 if side == 0 else -1
        return remote(part.at[block], full.at[side], y_send.at[2 + side], y_recv.at[2 + side], w, north(step))

    def across_cores(d):
        block = block_of(d)

        @pl.when(block % NC != c)
        def _():
            pair_copy(block).start()

    def from_core(d):
        block = block_of(d)
        r = away_of(block)

        @pl.when(block % NC == c)
        def _():
            pair_copy(block).wait_recv()
            part[block] += pair[r]

        @pl.when((block % NC == c) & (r == 2))
        def _():
            half_copy(0, block).start()
            half_copy(1, block).start()

    def to_owner(d):
        block = block_of(d)
        r = away_of(block)
        for side in range(2):

            @pl.when((block % NC == c) & (r == (1, 3)[side]))
            def _():
                half_copy(side, block).wait_recv()
                part[block, :, lanes[side]] += half[side]
                full_copy(side, block).start()

    for d in range(9):
        for side in range(2 if d < 7 else 0):
            if d > 0:
                z_arrival(side, d).wait_recv()
            z_copy(side, d).start()
            if d > 0:
                q, dz = events[d][side]
                x_copy(0, q, dz).start()
                x_copy(1, q, dz).start()
        if d == 7:
            for side in range(2):
                z_arrival(side, d).wait_recv()
        if d == 8:
            z_arrival(0, 8, top).wait_recv()
            z_arrival(1, 8, bottom).wait_recv()
        if d == 7:
            z_copy(0, 7, top).start()
            z_copy(1, 7, bottom).start()
        for q, dz in events[d] if d in (0, 7, 8) else ():
            for side in range(2):
                x_copy(side, q, dz).start()
        if d == 0:
            bundle_arrival(1).wait_recv()
            relay_start(1, 0, 5)
        if d == 1:
            relay_start(1, 5, 10)
        if d == 2:
            relay_start(1, 10, 15)
        if d == 3:
            bundle_arrival(3).wait_recv()
            relay_start(3, 0, 8)
        if d == 4:
            relay_start(3, 8, 15)
        if d == 5:
            bundle_arrival(2).wait_recv()
            relay_start(2, 0, 8)
        if d == 6:
            relay_start(2, 8, 15)
        if d >= 1:
            forward_x(d - 1)
        if d >= 2:
            last_x(d - 2)
        if d >= 3:
            product(d - 2)
        if d == 7:
            take_rows()
    forward_x(8)
    add_rows(1)
    across_cores(1)
    add_rows(2)
    across_cores(2)
    add_rows(3)
    across_cores(3)
    add_rows(4)
    across_cores(4)
    add_rows(5)
    across_cores(5)
    add_rows(6)
    across_cores(6)
    from_core(1)
    from_core(2)
    from_core(3)
    from_core(4)
    from_core(5)
    from_core(6)
    last_x(7)
    product(7)
    add_rows(7)
    across_cores(7)
    last_x(8)
    product(8)
    add_rows(8)
    across_cores(8)
    from_core(7)
    from_core(8)
    to_owner(1)
    to_owner(2)
    to_owner(3)
    to_owner(4)
    to_owner(5)
    to_owner(6)
    to_owner(7)
    to_owner(8)

    for side in range(2):
        full_copy(side, n).wait_recv()
    logits = part[n] + full[0] + full[1]

    def merged(buffer):
        peaks, masses = buffer[:, 0:1, :], buffer[:, 1:2, :]
        peak = jnp.max(peaks, axis=0)
        return peak, jnp.sum(masses * jnp.exp(peaks - peak[None]), axis=0)

    def put(buffer, index, peak, mass):
        buffer[index, 0:1, :] = peak
        buffer[index, 1:2, :] = mass

    peak = jnp.max(logits, axis=0, keepdims=True)
    mass = jnp.sum(jnp.exp(logits - peak), axis=0, keepdims=True)
    put(peaks_x, x, peak, mass)

    def sx_copy(k):
        return remote(peaks_x.at[x], peaks_x.at[x], sx_send.at[k], sx_recv.at[k], wide_of(0, k), n)

    for k in range(1, NX):
        sx_copy(k).start()
    for k in range(1, NX):
        sx_copy(k).wait_recv()
    peak, mass = merged(peaks_x)
    put(peaks_z, z, peak, mass)

    def sz_copy(k):
        return remote(peaks_z.at[z], peaks_z.at[z], sz_send.at[k], sz_recv.at[k], wide_of(k, 0), n)

    for k in FAR:
        sz_copy(k).start()
    for k in range(1, NZ):
        sz_copy(k).wait_recv()
    peak, mass = merged(peaks_z)
    o_ref[...] = logits - (peak + jnp.log(mass))

    for k in range(1, NN):
        sq_copy(k).wait_send()
    for k in range(1, NX):
        bundle_copy(k).wait_send()
    pltpu.make_async_copy(recv_rows.at[pl.ds(0, 60)], recv_rows.at[pl.ds(0, 60)], a2a_send).wait()
    pltpu.make_async_copy(act.at[pl.ds(0, 15)], act.at[pl.ds(0, 15)], z_send).wait()
    pltpu.make_async_copy(act.at[pl.ds(0, 32)], act.at[pl.ds(0, 32)], x_send).wait()
    pltpu.make_async_copy(act.at[pl.ds(0, 16)], act.at[pl.ds(0, 16)], h_send).wait()
    for r in range(NY):
        pair_copy(((y + r) % NY) * NC + 1 - c).wait_send()
    for side in range(2):
        half_copy(side, n).wait_send()
        full_copy(side, n).wait_send()
    for k in range(1, NX):
        sx_copy(k).wait_send()
    for k in range(1, NZ):
        sz_copy(k).wait_send()


def body(hidden, norm_gain, head_weight, diff_rows, slot_request, slot_code, slot_count):
    dma = pltpu.SemaphoreType.DMA
    vmem = pl.BlockSpec(memory_space=pltpu.VMEM)
    out = pl.pallas_call(
        head_kernel,
        name="head",
        out_shape=jax.ShapeDtypeStruct((VOC, ROWS), f32),
        in_specs=[vmem] * 7,
        out_specs=vmem,
        scratch_shapes=[
            pltpu.VMEM((NW, REQ, D // NN), bf16),
            pltpu.VMEM((NX, NZ, CAP, PADV), bf16),
            pltpu.VMEM((NX, NZ, CAP, PADV), bf16),
            pltpu.VMEM((NW, CAP, PADV), bf16),
            pltpu.VMEM((PADV, SLOTS), bf16),
            pltpu.VMEM((NN, VOC, ROWS), f32),
            pltpu.VMEM((NY, VOC, ROWS), f32),
            pltpu.VMEM((2, VOC, ROWS // 2), f32),
            pltpu.VMEM((2, VOC, ROWS), f32),
            pltpu.VMEM((NN, 1, 128), f32),
            pltpu.VMEM((NX, 2, ROWS), f32),
            pltpu.VMEM((NZ, 2, ROWS), f32),
            dma((NN,)), dma((NN,)), dma((NX,)), dma((NX,)), dma, dma, dma, dma((2, 9)), dma, dma((2, 16)), dma, dma((2, 16)),
            dma((NY,)), dma((NY,)), dma((4,)), dma((4,)), dma((NX,)), dma((NX,)), dma((NZ,)), dma((NZ,)),
        ],
        compiler_params=pltpu.CompilerParams(has_side_effects=True, collective_id=0, vmem_limit_bytes=40 << 20),
    )(
        hidden,
        norm_gain[None, :],
        head_weight.T,
        diff_rows[0, 0],
        jnp.transpose(slot_request, (1, 2, 0)),
        jnp.transpose(slot_code, (1, 2, 0)),
        slot_count.T,
    )
    return out.T


def solution(mesh):
    placed = (
        P("wide", "narrow"),
        P("narrow"),
        P("narrow", "wide"),
        P("wide", "narrow", None, None),
        P(),
        P(),
        P(),
    )
    return jax.shard_map(
        body, mesh=mesh, in_specs=placed, out_specs=P("narrow", "wide"), check_vma=False
    )
```
